32 devices in a mesh: tm: 4 (over z), node: 8 (over y, x, core).
Axes of the slice: x: 2, y: 2, z: 4, core: 2. Of those that a mesh axis runs over, the one named last changes fastest.
Arguments:
- memory: float32 [4096, 256], P('node'), may hold values from -6 to 6
- src_slot: int32 [4, 8, 512], P('tm', 'node'), may hold values from 0 to 1023, as said below
- dst_slot: int32 [4, 8, 512], P('tm', 'node'), may hold values from 0 to 1023, as said below
- event_time: float32 [4, 8, 512], P('tm', 'node'), may hold values from 0 to 200
- touched_rows: int32 [4, 8, 8, 128], P('tm', 'node'), may hold values from 0 to 511, as said below
- time_freq: float32 [128], replicated, may hold values from 0.01 to 1
- msg_weight: bfloat16 [640, 256], replicated, may hold values from -0.25 to 0.25
- msg_bias: float32 [256], replicated, may hold values from -3 to 3
- gate_weight: bfloat16 [256, 512], replicated, may hold values from -0.375 to 0.375
- update_bias: float32 [256], replicated, may hold values from -5 to 1
Outputs:
- period_memory: float32 [4, 4096, 256], P('tm', 'node')
The draws below stay inside these ranges and needn't reach their ends.
Inputs may be any that keep to these rules, and one draw needn't show every extreme that they name: touched_rows[t, o, b] holds 128 distinct rows among the 512 rows that owner o keeps. `src_slot`: slot s of event block b in period t stands for node (s // 128) * 512 + touched_rows[t, s // 128, b, s % 128]. `dst_slot`: read as src_slot.
All inputs are finite; a program needn't handle non-finite values.
Results may differ from the reference program's by a relative error of at most 0.0019.
Values may be sent and summed in bfloat16 or wider, within the bound.
No kernel may reach another device: no remote copies, remote signals or barrier semaphores. Data moves between devices by JAX's collectives and lax.ppermute only.
A program may use at most 64 MiB of HBM per device.

```python
import math
import jax
import jax.numpy as jnp
from jax import lax

MW = 256
TW = 128
CAP = 128
NODE_DEV = 512
EV_DEV = 512
PERIODS = 4
BLOCKS = 8
NODES = 4096


def slot_counts(base_key):
    count_key, owner_key, request_key = jax.random.split(jax.random.fold_in(base_key, 7), 3)
    counts = jax.random.randint(count_key, (PERIODS, BLOCKS, BLOCKS), CAP // 4, CAP + 1)
    requester = jnp.arange(BLOCKS)[None, None, :]
    full_one = jax.random.randint(owner_key, (PERIODS, BLOCKS, 1), 0, BLOCKS)
    counts = jnp.where(requester == full_one, CAP, counts)
    full_all = jax.random.randint(request_key, (PERIODS, 1, 1), 0, BLOCKS)
    counts = jnp.where(requester == full_all, CAP, counts)
    return counts


def event_slots(base_key, salt_value):
    counts = slot_counts(base_key)
    first_key, second_key, turn_key, place_key = jax.random.split(jax.random.fold_in(base_key, salt_value), 4)
    shape = (PERIODS, BLOCKS, EV_DEV)
    first_pick = jax.random.randint(first_key, shape, 0, BLOCKS)
    second = jax.random.randint(second_key, shape, 0, BLOCKS)
    rotation = jax.random.randint(turn_key, (PERIODS, 1, 1), 0, BLOCKS)
    owner_id = (jnp.minimum(first_pick, second) + rotation) % BLOCKS
    period_ids = jnp.arange(PERIODS)[:, None, None]
    block_ids = jnp.arange(BLOCKS)[None, :, None]
    limits = counts[period_ids, owner_id, block_ids]
    position = jax.random.randint(place_key, shape, 0, limits)
    return (owner_id * CAP + position).astype(jnp.int32)


def draw_src_slot(key, part):
    return event_slots(key, 21)


def draw_dst_slot(key, part):
    return event_slots(key, 22)


def draw_touched_rows(key, part):
    random_bits = jax.random.randint(jax.random.fold_in(key, 11), (PERIODS, BLOCKS, BLOCKS, NODE_DEV), 0, 1 << 16)
    scores = random_bits * NODE_DEV + jnp.arange(NODE_DEV)
    ordering = jnp.argsort(scores, axis=-1)
    return ordering[..., :CAP].astype(jnp.int32)


def steps_of(stream_key, shape, cuts, smallest, high):
    def one(dim, parts):
        heights = jax.random.uniform(jax.random.fold_in(jax.random.fold_in(stream_key, 6), dim), (parts,), jnp.float32, smallest / len(cuts), high / len(cuts))
        return jnp.repeat(jnp.exp(heights), shape[dim] // parts).reshape((-1,) + (1,) * (len(shape) - dim - 1))

    gain = one(*cuts[0])
    for cut in cuts[1:]:
        gain = gain * one(*cut)
    return gain


def gaussian(own_key, dims, spread, most, cuts=(), held_as=jnp.bfloat16):
    drawn = spread * jax.random.normal(own_key, dims, jnp.float32)
    if cuts:
        drawn = drawn * steps_of(own_key, dims, cuts, -0.22, 0.18)
    return jnp.clip(drawn, -most, most).astype(held_as)


def setup_inputs(seed: int = 0) -> dict:
    splits = jax.random.split(jax.random.key(seed), 11)
    memory = gaussian(splits[0], (NODES, MW), 1.0, 6.0, ((0, 8),), jnp.float32)
    src_slot = draw_src_slot(jax.random.fold_in(splits[10], 71), 0)
    dst_slot = draw_dst_slot(jax.random.fold_in(splits[10], 71), 0)
    event_time = jnp.clip(200.0 * jax.random.uniform(splits[3], (PERIODS, BLOCKS, EV_DEV), jnp.float32) ** steps_of(splits[3], (PERIODS, BLOCKS, EV_DEV), ((0, 4), (1, 8)), -0.2, 0.2), 0.0, 200.0)
    touched_rows = draw_touched_rows(jax.random.fold_in(splits[10], 71), 0)
    time_freq = jnp.clip(jnp.exp(jax.random.uniform(splits[5], (TW,), jnp.float32, math.log(0.01), math.log(1.0))), 0.01, 1.0)
    msg_weight = gaussian(splits[6], (2 * MW + TW, MW), (2 * MW + TW) ** -0.5, 0.25)
    msg_bias = gaussian(splits[7], (MW,), 0.5, 3.0, (), jnp.float32)
    gate_weight = gaussian(splits[8], (MW, 2 * MW), MW ** -0.5, 0.375)
    update_bias = jnp.clip(jax.random.uniform(splits[9], (MW,), jnp.float32, -5.0, 1.0), -5.0, 1.0)
    return {"memory": memory, "src_slot": src_slot, "dst_slot": dst_slot, "event_time": event_time, "touched_rows": touched_rows, "time_freq": time_freq, "msg_weight": msg_weight, "msg_bias": msg_bias, "gate_weight": gate_weight, "update_bias": update_bias}


def reference(memory, src_slot, dst_slot, event_time, touched_rows, time_freq, msg_weight, msg_bias, gate_weight, update_bias):
    capacity = touched_rows.shape[3]
    total_nodes = memory.shape[0]
    node_rows = total_nodes // src_slot.shape[1]
    breadth = memory.shape[1]
    rounded = lax.optimization_barrier(memory.astype(jnp.bfloat16)).astype(memory.dtype)
    weight_wide = msg_weight.astype(memory.dtype)
    gate_wide = gate_weight.astype(memory.dtype)

    def node_lookup(slot_ids, slot_table):
        owner_id = (slot_ids // capacity).astype(jnp.int32)
        position = (slot_ids % capacity).astype(jnp.int32)
        return slot_table[owner_id, position] + owner_id * node_rows

    def one_block(running, pieces):
        totals, counts = running
        sources, targets, event_times, slot_table = pieces
        src_node = node_lookup(sources, slot_table)
        dst_node = node_lookup(targets, slot_table)
        from_rows = rounded[src_node]
        to_rows = rounded[dst_node]
        encoding = jnp.cos(event_times[:, None] * time_freq[None, :])
        encoding = lax.optimization_barrier(encoding.astype(jnp.bfloat16)).astype(memory.dtype)
        inputs = jnp.concatenate([
            jnp.concatenate([from_rows, to_rows, encoding], 1),
            jnp.concatenate([to_rows, from_rows, encoding], 1)], 0)
        messages = jax.nn.relu(jnp.dot(inputs, weight_wide, precision=lax.Precision.HIGHEST) + msg_bias)
        all_nodes = jnp.concatenate([src_node, dst_node])
        totals = totals.at[all_nodes].add(messages)
        counts = counts.at[all_nodes].add(jnp.ones(all_nodes.shape, memory.dtype))
        return (totals, counts), None

    def one_period(memory_state, period_data):
        sources, targets, event_times, row_lists = period_data
        zero_sums = (jnp.zeros_like(memory), jnp.zeros((total_nodes,), memory.dtype))
        (totals, counts), unused = lax.scan(one_block, zero_sums, (sources, targets, event_times, jnp.swapaxes(row_lists, 0, 1)))
        mean_msg = totals / jnp.maximum(counts, 1.0)[:, None]
        mean_msg = lax.optimization_barrier(mean_msg.astype(jnp.bfloat16)).astype(memory.dtype)
        gate_terms = jnp.dot(mean_msg, gate_wide, precision=lax.Precision.HIGHEST)
        update = jax.nn.sigmoid(gate_terms[:, :breadth] + update_bias)
        candidate = jnp.tanh(gate_terms[:, breadth:])
        touched = (counts > 0.0)[:, None]
        keep_rate = jnp.where(touched, 1.0 - update, 1.0)
        write_term = jnp.where(touched, update * candidate, 0.0)
        updated = keep_rate * memory_state + write_term
        return updated, updated

    final_state, history = lax.scan(one_period, memory, (src_slot, dst_slot, event_time, touched_rows))
    return history
```

```python
import jax
import jax.numpy as jnp
from jax import lax
from jax.sharding import PartitionSpec as P


def xor_permuted(values, index):
    count = values.shape[0]
    step = 1
    while step < count:
        pairs = values.reshape((count // (2 * step), 2, step) + values.shape[1:])
        swapped = jnp.flip(pairs, 1).reshape(values.shape)
        values = jnp.where((index // step) % 2 == 1, swapped, values)
        step *= 2
    return values


def hubs_of(periods):
    return (periods - 1) // 2, (periods - 1) // 2 + 1


def rounds_of(first, second):
    second = second[1:] + second[:1]
    longest = max(len(first), len(second))
    first = first + [None] * (longest - len(first))
    second = second + [None] * (longest - len(second))
    return list(zip(first, second))


def node_swap(value, distance):
    size = lax.axis_size("node")
    return lax.ppermute(value, "node", [(i, i ^ distance) for i in range(size)])


def hot_columns(indices, height):
    return (jnp.arange(height, dtype=jnp.int32)[:, None] == indices[None, :]).astype(jnp.bfloat16)


def gates(mean_code, gate_weight, update_bias):
    breadth = mean_code.shape[1]
    terms = jnp.dot(mean_code, gate_weight, preferred_element_type=jnp.float32)
    update = jax.nn.sigmoid(terms[:, :breadth] + update_bias)
    candidate = jnp.tanh(terms[:, breadth:])
    touched = mean_code >= 0
    keep_rate = jnp.where(touched, 1.0 - update, 1.0)
    write_term = jnp.where(touched, update * candidate, 0.0)
    return keep_rate, write_term


def shards(
    memory,
    src_slot,
    dst_slot,
    event_time,
    touched_rows,
    time_freq,
    msg_weight,
    msg_bias,
    gate_weight,
    update_bias,
):
    me = lax.axis_index("node")
    period = lax.axis_index("tm")
    periods = lax.axis_size("tm")
    blocks, capacity = touched_rows.shape[2:]
    node_rows, breadth = memory.shape
    chips = blocks // 2
    lists = xor_permuted(touched_rows[0, 0], me)
    row_hot = hot_columns(lists.reshape(-1), node_rows)
    hot_by = row_hot.reshape(node_rows, chips, 2, capacity)
    stale = memory.astype(jnp.bfloat16)

    def picked(hot):
        rows = lax.dot_general(
            hot.reshape(node_rows, -1), stale, (((0,), (0,)), ((), ())),
            preferred_element_type=jnp.float32,
        )
        return rows.astype(jnp.bfloat16).reshape(chips, capacity, breadth)

    other = picked(hot_by[:, :, 1])
    from_partner = node_swap(other, 1)
    own = picked(hot_by[:, :, 0])
    tables = [own[0], from_partner[0]]
    for chip in range(chips - 1, 0, -1):
        pair = jnp.stack([own[chip], from_partner[chip]])
        tables.append((chip, node_swap(pair, 2 * chip)))
    tables = tables[:2] + [piece for _, pair in sorted(tables[2:], key=lambda x: x[0]) for piece in pair]
    slot_table = jnp.concatenate(tables, 0)

    slots = jnp.concatenate([src_slot[0, 0], dst_slot[0, 0]])
    slots = ((slots // capacity) ^ me) * capacity + slots % capacity
    events = slots.shape[0] // 2
    slot_hot = hot_columns(slots, blocks * capacity)
    counts = jnp.sum(slot_hot, axis=1, dtype=jnp.float32).reshape(chips, 2, capacity)
    partner_counts = node_swap(counts[:, 1], 1)
    both_rows = lax.dot_general(
        slot_hot, slot_table, (((0,), (0,)), ((), ())), preferred_element_type=jnp.float32
    ).astype(jnp.bfloat16)
    from_rows, to_rows = both_rows[:events], both_rows[events:]
    encoding = jnp.cos(event_time[0, 0][:, None] * time_freq[None, :]).astype(jnp.bfloat16)
    inputs = jnp.concatenate(
        [
            jnp.concatenate([from_rows, to_rows, encoding], 1),
            jnp.concatenate([to_rows, from_rows, encoding], 1),
        ],
        0,
    )
    messages = jax.nn.relu(
        jnp.dot(inputs, msg_weight, preferred_element_type=jnp.float32) + msg_bias
    ).astype(jnp.bfloat16)
    hot_slots = slot_hot.reshape(chips, 2, capacity, 2 * events)

    def summed(hot):
        sums = jnp.dot(hot.reshape(-1, 2 * events), messages, preferred_element_type=jnp.float32)
        return sums.astype(jnp.bfloat16).reshape(chips, capacity, breadth)

    other_sums = summed(hot_slots[:, 1])
    partner_sums = node_swap(other_sums, 1)
    own_sums = summed(hot_slots[:, 0])
    base = 32.0
    got_sums = [None] * blocks
    got_counts = [None] * blocks
    got_sums[:2] = [own_sums[0], partner_sums[0]]
    got_counts[:2] = [counts[0, 0], partner_counts[0]]
    code_rows = -(-4 * capacity // breadth)
    for chip in range(chips - 1, 0, -1):
        code = jnp.stack([counts[chip, 0], partner_counts[chip]])
        upper = jnp.floor(code * (1.0 / base))
        code = jnp.concatenate([upper, code - base * upper], 0).reshape(-1)
        code = jnp.pad(code, (0, code_rows * breadth - code.shape[0])).reshape(code_rows, breadth)
        load = jnp.concatenate(
            [own_sums[chip], partner_sums[chip], code.astype(jnp.bfloat16)], 0
        )
        got = node_swap(load, 2 * chip)
        code = got[2 * capacity:].astype(jnp.float32).reshape(-1)[: 4 * capacity]
        code = code.reshape(4, capacity)
        for side in range(2):
            got_sums[2 * chip + side] = got[side * capacity : (side + 1) * capacity]
            got_counts[2 * chip + side] = base * code[side] + code[2 + side]

    totals = jnp.dot(row_hot, jnp.concatenate(got_sums, 0), preferred_element_type=jnp.float32)
    count_all = jnp.concatenate(got_counts)
    node_counts = jnp.sum(
        jnp.where(row_hot > 0, count_all[None, :], 0.0), axis=1, keepdims=True
    )
    mean_code = jnp.where(
        node_counts > 0.0, totals / jnp.maximum(node_counts, 1.0), -1.0
    ).astype(jnp.bfloat16)

    half = node_rows // 2
    hub_low, hub_high = hubs_of(periods)
    is_high = period == hub_high
    sources_low = [t for t in range(periods - 1) if t != hub_low]
    sources_high = [t for t in range(periods - 1) if t != hub_high]
    got_means = []
    came = rounds_of(sources_low, sources_high)
    for low, high in came:
        pairs = [(s, h) for s, h in ((low, hub_low), (high, hub_high)) if s is not None]
        start = jnp.where(period == (-1 if high is None else high), half, 0)
        got_means.append(
            lax.ppermute(lax.dynamic_slice_in_dim(mean_code, start, half, 0), "tm", pairs)
        )
    keep, write = gates(mean_code, gate_weight, update_bias)
    start = jnp.where(is_high, half, 0)
    state = lax.dynamic_slice_in_dim(memory, start, half, 0)
    own_keep = lax.dynamic_slice_in_dim(keep, start, half, 0)
    own_write = lax.dynamic_slice_in_dim(write, start, half, 0)
    came_gates = [gates(mean, gate_weight, update_bias) for mean in got_means]
    states = []
    for t in range(periods - 1):
        low = next((g for g, r in zip(came_gates, came) if r[0] == t), (own_keep, own_write))
        high = next((g for g, r in zip(came_gates, came) if r[1] == t), (own_keep, own_write))
        rate, term = (jnp.where(is_high, b, a) for a, b in zip(low, high))
        state = rate * state + term
        states.append(state)
    targets_low = [t for t in range(1, periods) if t != hub_low]
    targets_high = [t for t in range(1, periods) if t != hub_high]
    before_low = jnp.where(period == 0, memory[:half], states[max(hub_low - 1, 0)])
    before_high = jnp.where(period == 0, memory[half:], states[hub_high - 1])
    for low, high in rounds_of(targets_low, targets_high):
        pairs = [(h, d) for d, h in ((low, hub_low), (high, hub_high)) if d is not None]
        low_state = states[(high if low is None else low) - 1]
        high_state = states[(low if high is None else high) - 1]
        sent = jnp.where(is_high, high_state, low_state).astype(jnp.float16)
        got = lax.ppermute(sent, "tm", pairs).astype(jnp.float32)
        if low is not None:
            before_low = jnp.where(period == low, got, before_low)
        if high is not None:
            before_high = jnp.where(period == high, got, before_high)
    before = jnp.concatenate([before_low, before_high], 0)
    return (keep * before + write)[None]


def solution(mesh):
    return jax.shard_map(
        shards,
        mesh=mesh,
        in_specs=(
            P("node", None),
            P("tm", "node", None),
            P("tm", "node", None),
            P("tm", "node", None),
            P("tm", "node", None, None),
            P(),
            P(),
            P(),
            P(),
            P(),
        ),
        out_specs=P("tm", "node", None),
        check_vma=False,
    )
```

```python
import functools

import jax
import jax.numpy as jnp
from jax import lax
from jax.experimental import pallas as pl
from jax.experimental.pallas import tpu as pltpu
from jax.sharding import PartitionSpec as P

PIECES = 2
BASE = 32.0
VMEM_LIMIT = 20 << 20
F32 = jnp.float32
BF16 = jnp.bfloat16


def dot(a, b, dims=((1,), (0,))):
    return lax.dot_general(a, b, (dims, ((), ())), preferred_element_type=F32)


def call(kernel, outs, *args, flops=0):
    outs = [jax.ShapeDtypeStruct(shape, dtype) for shape, dtype in outs]
    moved = sum(x.size * x.dtype.itemsize for x in [*args, *outs])
    return pl.pallas_call(
        kernel,
        out_shape=outs,
        in_specs=[pl.BlockSpec(memory_space=pltpu.VMEM)] * len(args),
        out_specs=[pl.BlockSpec(memory_space=pltpu.VMEM)] * len(outs),
        cost_estimate=pl.CostEstimate(flops=flops, bytes_accessed=moved, transcendentals=0),
        compiler_params=pltpu.CompilerParams(vmem_limit_bytes=VMEM_LIMIT),
    )(*args)


def columns_of(row):
    return jnp.transpose(jnp.broadcast_to(row, (row.shape[1], row.shape[1])))


def hot_rows(row, width):
    count = row.shape[1]
    column = jnp.concatenate([columns_of(row)] * (width // count), 1)
    lanes = lax.broadcasted_iota(jnp.int32, (count, width), 1)
    return jnp.where(column == lanes, 1.0, 0.0).astype(BF16)


def hot_columns(row, start, height):
    sublanes = lax.broadcasted_iota(jnp.int32, (height, row.shape[1]), 0) + start
    return jnp.where(row == sublanes, 1.0, 0.0).astype(BF16)


def pick_kernel(side, lists_ref, memory_ref, out_ref):
    me = lax.axis_index("node")
    stale = memory_ref[...].astype(BF16)
    for chip in range(out_ref.shape[0]):
        row = lists_ref[pl.ds(me ^ (2 * chip + side), 1), :]
        hot = hot_rows(row, memory_ref.shape[0])
        out_ref[chip] = dot(hot, stale).astype(BF16)


def prep_kernel(
    slots_ref, time_ref, freq_ref, weight_ref, bias_ref, hot_ref, turned_ref, base_ref, code_ref
):
    me = lax.axis_index("node")
    slots_all, ends = hot_ref.shape
    blocks, capacity = code_ref.shape[0], code_ref.shape[2] // 2
    slots = slots_ref[...]
    slots = ((slots // capacity) ^ me) * capacity + slots % capacity
    counts = jnp.zeros((8, slots_all), F32)
    ones = jnp.ones((8, capacity), BF16)
    for i in range(ends // capacity):
        rows = slice(i * capacity, (i + 1) * capacity)
        turned = hot_rows(slots[:, rows], slots_all)
        turned_ref[rows] = turned
        counts = counts + dot(ones, turned)
    for j in range(blocks):
        hot_ref[j * capacity : (j + 1) * capacity] = hot_columns(slots, j * capacity, capacity)
    upper = jnp.floor(counts * (1.0 / BASE))
    lower = counts - BASE * upper
    for j in range(blocks):
        lanes = slice(j * capacity, (j + 1) * capacity)
        code = jnp.concatenate([upper[:, lanes], lower[:, lanes]], 1)
        code_ref[j] = code[: code_ref.shape[1]].astype(BF16)
    width = freq_ref.shape[1]
    stale_part = weight_ref.shape[0] - width
    for i in range(time_ref.shape[1] // width):
        rows = slice(i * width, (i + 1) * width)
        encoding = jnp.cos(columns_of(time_ref[:, rows]) * freq_ref[...]).astype(BF16)
        base_ref[rows] = dot(encoding, weight_ref[stale_part:]) + bias_ref[...]


def message_kernel(chips, *refs):
    tables, (turned_ref, hot_ref, weight_ref, base_ref, code_ref) = refs[:-7], refs[-7:-2]
    other_ref, message_ref = refs[-2:]
    capacity, breadth = tables[0].shape
    rows = None
    for j, table in enumerate(tables[:2]):
        part = dot(turned_ref[:, j * capacity : (j + 1) * capacity], table[...])
        rows = part if rows is None else rows + part
    for chip in range(1, chips):
        lanes = slice(2 * chip * capacity, 2 * (chip + 1) * capacity)
        table = tables[chip + 1][...].reshape(2 * capacity, breadth)
        rows = rows + dot(turned_ref[:, lanes], table)
    rows = rows.astype(BF16)
    events = rows.shape[0] // 2
    first = dot(rows, weight_ref[:breadth])
    second = dot(rows, weight_ref[breadth : 2 * breadth])
    base = base_ref[...]
    message_ref[:events] = jnp.maximum(first[:events] + second[events:] + base, 0.0).astype(BF16)
    message_ref[events:] = jnp.maximum(first[events:] + second[:events] + base, 0.0).astype(BF16)
    messages = message_ref[...]
    for chip in range(chips):
        j = 2 * chip + 1
        sums = dot(hot_ref[j * capacity : (j + 1) * capacity], messages)
        other_ref[chip, :capacity] = sums.astype(BF16)
        other_ref[chip, capacity:] = code_ref[j]


def own_kernel(hot_ref, message_ref, own_ref):
    messages = message_ref[...]
    chips, capacity, _ = own_ref.shape
    for chip in range(chips):
        rows = slice(2 * chip * capacity, (2 * chip + 1) * capacity)
        own_ref[chip] = dot(hot_ref[rows], messages).astype(BF16)


def rows_kernel(lists_ref, rowhot_ref):
    me = lax.axis_index("node")
    blocks, capacity = lists_ref.shape
    for j in range(blocks):
        row = lists_ref[pl.ds(me ^ j, 1), :]
        rowhot_ref[:, j * capacity : (j + 1) * capacity] = hot_columns(
            row, 0, rowhot_ref.shape[0]
        )


def mean_kernel(chips, rowhot_ref, *refs):
    loads, mean_ref = refs[:-1], refs[-1]
    breadth = mean_ref.shape[1]
    pair = rowhot_ref.shape[1] // chips
    capacity = pair // 2
    totals, counts = None, None
    for chip, load in enumerate(loads):
        hot = rowhot_ref[:, chip * pair : (chip + 1) * pair]
        part = dot(hot, load[:pair])
        first = load[pair : pair + 1].astype(F32)
        second = load[pair + 1 : pair + 2].astype(F32)
        upper = jnp.concatenate([first[:, :capacity], second[:, :capacity]], 1)
        lower = jnp.concatenate([first[:, capacity:], second[:, capacity:]], 1)
        code = jnp.concatenate(
            [
                jnp.broadcast_to(upper, (breadth // 2, pair)),
                jnp.broadcast_to(lower, (breadth // 2, pair)),
            ],
            0,
        ).astype(BF16)
        count = dot(hot, code, ((1,), (1,)))
        totals = part if totals is None else totals + part
        counts = count if counts is None else counts + count
    counts = BASE * counts[:, : breadth // 2] + counts[:, breadth // 2 :]
    counts = jnp.concatenate([counts, counts], 1)
    mean = jnp.where(counts > 0.0, totals / jnp.maximum(counts, 1.0), -1.0)
    mean_ref[...] = mean.astype(BF16)


def gates(mean_code, gate_weight, update_bias):
    breadth = mean_code.shape[1]
    terms = dot(mean_code, gate_weight)
    update = jax.nn.sigmoid(terms[:, :breadth] + update_bias)
    candidate = jnp.tanh(terms[:, breadth:])
    touched = mean_code.astype(F32) >= 0.0
    keep_rate = jnp.where(touched, 1.0 - update, 1.0)
    write_term = jnp.where(touched, update * candidate, 0.0)
    return keep_rate, write_term


def hubs_of(periods):
    return (periods - 1) // 2, (periods - 1) // 2 + 1


def rounds_of(first, second):
    second = second[1:] + second[:1]
    longest = max(len(first), len(second))
    first = first + [None] * (longest - len(first))
    second = second + [None] * (longest - len(second))
    return list(zip(first, second))


def plan_of(periods):
    low, high = hubs_of(periods)
    came = rounds_of(
        [t for t in range(periods - 1) if t != low], [t for t in range(periods - 1) if t != high]
    )
    went = rounds_of(
        [t for t in range(1, periods) if t != low], [t for t in range(1, periods) if t != high]
    )
    return low, high, came, went


def hub_kernel(periods, own_ref, memory_ref, weight_ref, bias_ref, *refs):
    hub_low, hub_high, came, went = plan_of(periods)
    means, outs = refs[: len(came)], refs[len(came) :]
    is_high = lax.axis_index("tm") == hub_high
    own_gates = gates(own_ref[...], weight_ref[...], bias_ref[...])
    came_gates = [gates(mean[...], weight_ref[...], bias_ref[...]) for mean in means]
    state = memory_ref[...]
    states = []
    for t in range(periods - 1):
        low = next((g for g, r in zip(came_gates, came) if r[0] == t), own_gates)
        high = next((g for g, r in zip(came_gates, came) if r[1] == t), own_gates)
        rate, term = (jnp.where(is_high, b, a) for a, b in zip(low, high))
        state = rate * state + term
        states.append(state)
    for (low, high), out in zip(went, outs):
        low_state = states[(high if low is None else low) - 1]
        high_state = states[(low if high is None else high) - 1]
        out[...] = jnp.where(is_high, high_state, low_state)
    outs[-1][...] = jnp.where(is_high, states[hub_high - 1], states[max(hub_low - 1, 0)])


def node_swap(value, distance):
    size = lax.axis_size("node")
    return lax.ppermute(value, "node", [(i, i ^ distance) for i in range(size)])


def shards(
    memory,
    src_slot,
    dst_slot,
    event_time,
    touched_rows,
    time_freq,
    msg_weight,
    msg_bias,
    gate_weight,
    update_bias,
):
    period = lax.axis_index("tm")
    periods = lax.axis_size("tm")
    blocks, capacity = touched_rows.shape[2:]
    node_rows, breadth = memory.shape
    events = src_slot.shape[2]
    chips = blocks // 2
    lists = touched_rows[0, 0]

    def picked(side):
        return call(
            functools.partial(pick_kernel, side),
            [((chips, capacity, breadth), BF16)],
            lists,
            memory,
            flops=chips * capacity * breadth * node_rows * 2,
        )[0]

    from_partner = node_swap(picked(1), 1)
    own = picked(0)
    sources, targets, times, from_partner = lax.optimization_barrier(
        (src_slot[0], dst_slot[0], event_time[0], from_partner)
    )
    tables = [own[0], from_partner[0]] + [
        node_swap(jnp.stack([own[chip], from_partner[chip]]), 2 * chip)
        for chip in range(1, chips)
    ]
    ends = 2 * events
    slots = blocks * capacity
    hot, turned, base, code = call(
        prep_kernel,
        [
            ((slots, ends), BF16),
            ((ends, slots), BF16),
            ((events, breadth), F32),
            ((blocks, 1, 2 * capacity), BF16),
        ],
        jnp.concatenate([sources, targets], 1),
        times,
        time_freq[None],
        msg_weight,
        msg_bias[None],
    )
    other, messages = call(
        functools.partial(message_kernel, chips),
        [((chips, capacity + 1, breadth), BF16), ((ends, breadth), BF16)],
        *tables,
        turned,
        hot,
        msg_weight,
        base,
        code,
        flops=ends * slots * breadth * 3,
    )
    partner = node_swap(other, 1)
    own_sums = call(
        own_kernel,
        [((chips, capacity, breadth), BF16)],
        hot,
        messages,
        flops=ends * slots * breadth,
    )[0]
    loads = []
    for chip in range(chips):
        load = jnp.concatenate(
            [own_sums[chip], partner[chip, :capacity], code[2 * chip], partner[chip, capacity:]], 0
        )
        loads.append(node_swap(load, 2 * chip) if chip else load)
    rowhot = call(rows_kernel, [((node_rows, slots), BF16)], lists)[0]
    mean_code = call(
        functools.partial(mean_kernel, chips),
        [((node_rows, breadth), BF16)],
        rowhot,
        *loads,
        flops=4 * node_rows * slots * breadth,
    )[0]

    half = node_rows // 2
    size = half // PIECES
    hub_low, hub_high, came, went = plan_of(periods)
    is_high = period == hub_high
    bias = update_bias[None]
    got_means = []
    for piece in range(PIECES):
        got = []
        for low, high in came:
            pairs = [(s, h) for s, h in ((low, hub_low), (high, hub_high)) if s is not None]
            start = jnp.where(period == (-1 if high is None else high), half, 0) + piece * size
            sent = lax.dynamic_slice_in_dim(mean_code, start, size, 0)
            got.append(lax.ppermute(sent, "tm", pairs))
        got_means.append(got)
    keep, write = gates(mean_code, gate_weight, bias)
    before_low, before_high = [], []
    for piece in range(PIECES):
        start = jnp.where(is_high, half, 0) + piece * size
        outs = call(
            functools.partial(hub_kernel, periods),
            [((size, breadth), F32)] * (len(went) + 1),
            lax.dynamic_slice_in_dim(mean_code, start, size, 0),
            lax.dynamic_slice_in_dim(memory, start, size, 0),
            gate_weight,
            bias,
            *got_means[piece],
            flops=2 * (len(came) + 1) * size * breadth * breadth * 2,
        )
        first = piece * size
        prior_low = jnp.where(period == 0, memory[first : first + size], outs[-1])
        first += half
        prior_high = jnp.where(period == 0, memory[first : first + size], outs[-1])
        for r, (low, high) in enumerate(went):
            pairs = [(h, d) for d, h in ((low, hub_low), (high, hub_high)) if d is not None]
            got = lax.ppermute(outs[r].astype(jnp.float16), "tm", pairs)
            got = got.astype(F32)
            if low is not None:
                prior_low = jnp.where(period == low, got, prior_low)
            if high is not None:
                prior_high = jnp.where(period == high, got, prior_high)
        before_low.append(prior_low)
        before_high.append(prior_high)
    before = jnp.concatenate(before_low + before_high, 0)
    return (keep * before + write)[None]


def solution(mesh):
    return jax.shard_map(
        shards,
        mesh=mesh,
        in_specs=(
            P("node", None),
            P("tm", "node", None),
            P("tm", "node", None),
            P("tm", "node", None),
            P("tm", "node", None, None),
            P(),
            P(),
            P(),
            P(),
            P(),
        ),
        out_specs=P("tm", "node", None),
        check_vma=False,
    )
```

```python
import jax
import jax.numpy as jnp
from jax import lax
from jax.experimental import pallas as pl
from jax.experimental.pallas import tpu as pltpu
from jax.sharding import PartitionSpec as P

BASE = 32.0
VMEM_LIMIT = 20 << 20
F32 = jnp.float32
BF16 = jnp.bfloat16


def dot(a, b, dims=((1,), (0,))):
    return lax.dot_general(a, b, (dims, ((), ())), preferred_element_type=F32)


def call(kernel, outs, *args, flops=0, scratch=(), raw_out=()):
    outs = [jax.ShapeDtypeStruct(shape, dtype) for shape, dtype in outs]
    moved = sum(x.size * x.dtype.itemsize for x in [*args, *outs])

    def specs(count, raw):
        return [
            pl.BlockSpec(memory_space=pl.ANY if i in raw else pltpu.VMEM) for i in range(count)
        ]

    return pl.pallas_call(
        kernel,
        out_shape=outs,
        in_specs=specs(len(args), ()),
        out_specs=specs(len(outs), raw_out),
        scratch_shapes=list(scratch),
        cost_estimate=pl.CostEstimate(flops=flops, bytes_accessed=moved, transcendentals=0),
        compiler_params=pltpu.CompilerParams(vmem_limit_bytes=VMEM_LIMIT),
    )(*args)


def columns_of(row):
    return jnp.transpose(jnp.broadcast_to(row, (row.shape[1], row.shape[1])))


def hot_rows(row, width):
    count = row.shape[1]
    column = jnp.concatenate([columns_of(row)] * (width // count), 1)
    lanes = lax.broadcasted_iota(jnp.int32, (count, width), 1)
    return jnp.where(column == lanes, 1.0, 0.0).astype(BF16)


def hot_columns(row, start, height):
    sublanes = lax.broadcasted_iota(jnp.int32, (height, row.shape[1]), 0) + start
    return jnp.where(row == sublanes, 1.0, 0.0).astype(BF16)


def fetch_kernel(lists_ref, memory_ref, out_ref, stale_ref):
    me = lax.axis_index("node")
    stale = memory_ref[...].astype(BF16)
    stale_ref[...] = stale
    for chip in range(out_ref.shape[0]):
        hot = hot_rows(lists_ref[pl.ds(me ^ (2 * chip + 1), 1), :], stale.shape[0])
        out_ref[chip] = dot(hot, stale).astype(BF16)


def pick_kernel(lists_ref, stale_ref, out_ref):
    me = lax.axis_index("node")
    stale = stale_ref[...]
    for chip in range(out_ref.shape[0]):
        hot = hot_rows(lists_ref[pl.ds(me ^ (2 * chip), 1), :], stale.shape[0])
        out_ref[chip] = dot(hot, stale).astype(BF16)


def prep_kernel(
    slots_ref, time_ref, freq_ref, weight_ref, bias_ref, hot_ref, turned_ref, base_ref, code_ref
):
    me = lax.axis_index("node")
    slots_all, ends = hot_ref.shape
    blocks, capacity = code_ref.shape[0], code_ref.shape[2] // 2
    slots = slots_ref[...]
    slots = ((slots // capacity) ^ me) * capacity + slots % capacity
    counts = jnp.zeros((8, slots_all), F32)
    ones = jnp.ones((8, capacity), BF16)
    for i in range(ends // capacity):
        rows = slice(i * capacity, (i + 1) * capacity)
        turned = hot_rows(slots[:, rows], slots_all)
        turned_ref[rows] = turned
        counts = counts + dot(ones, turned)
    for j in range(blocks):
        hot_ref[j * capacity : (j + 1) * capacity] = hot_columns(slots, j * capacity, capacity)
    upper = jnp.floor(counts * (1.0 / BASE))
    lower = counts - BASE * upper
    for j in range(blocks):
        lanes = slice(j * capacity, (j + 1) * capacity)
        code = jnp.concatenate([upper[:, lanes], lower[:, lanes]], 1)
        code_ref[j] = code[: code_ref.shape[1]].astype(BF16)
    width = freq_ref.shape[1]
    stale_part = weight_ref.shape[0] - width
    for i in range(time_ref.shape[1] // width):
        rows = slice(i * width, (i + 1) * width)
        encoding = jnp.cos(columns_of(time_ref[:, rows]) * freq_ref[...]).astype(BF16)
        base_ref[rows] = dot(encoding, weight_ref[stale_part:]) + bias_ref[...]


def gathered(turned_ref, start, tables):
    rows = None
    for table in tables:
        stop = start + table.shape[0]
        part = dot(turned_ref[:, start:stop], table)
        rows = part if rows is None else rows + part
        start = stop
    return rows


def gather_kernel(own_ref, partner_ref, near_ref, turned_ref, rows_ref):
    capacity, breadth = own_ref.shape
    tables = [
        jnp.concatenate([own_ref[...], partner_ref[...]], 0),
        near_ref[...].reshape(2 * capacity, breadth),
    ]
    rows_ref[...] = gathered(turned_ref, 0, tables)


def message_kernel(rows_ref, *refs):
    tables, (turned_ref, hot_ref, weight_ref, base_ref, code_ref) = refs[:-7], refs[-7:-2]
    other_ref, message_ref = refs[-2:]
    _, capacity, breadth = tables[0].shape
    tables = [table[...].reshape(2 * capacity, breadth) for table in tables]
    rows = (rows_ref[...] + gathered(turned_ref, 4 * capacity, tables)).astype(BF16)
    events = rows.shape[0] // 2
    first = dot(rows, weight_ref[:breadth])
    second = dot(rows, weight_ref[breadth : 2 * breadth])
    base = base_ref[...]
    message_ref[:events] = jnp.maximum(first[:events] + second[events:] + base, 0.0).astype(BF16)
    message_ref[events:] = jnp.maximum(first[events:] + second[:events] + base, 0.0).astype(BF16)
    messages = message_ref[...]
    for chip in range(other_ref.shape[0]):
        j = 2 * chip + 1
        sums = dot(hot_ref[j * capacity : (j + 1) * capacity], messages)
        other_ref[chip, :capacity] = sums.astype(BF16)
        other_ref[chip, capacity:] = code_ref[j]


def own_kernel(hot_ref, message_ref, own_ref):
    messages = message_ref[...]
    chips, capacity, _ = own_ref.shape
    for chip in range(chips):
        rows = slice(2 * chip * capacity, (2 * chip + 1) * capacity)
        own_ref[chip] = dot(hot_ref[rows], messages).astype(BF16)


def rows_kernel(lists_ref, rowhot_ref):
    me = lax.axis_index("node")
    blocks, capacity = lists_ref.shape
    for j in range(blocks):
        row = lists_ref[pl.ds(me ^ j, 1), :]
        rowhot_ref[:, j * capacity : (j + 1) * capacity] = hot_columns(
            row, 0, rowhot_ref.shape[0]
        )


def load_totals(rowhot_ref, start, loads):
    totals, counts = None, None
    for load in loads:
        breadth = load.shape[1]
        pair = 2 * (load.shape[0] // 2 - 1)
        capacity = pair // 2
        hot = rowhot_ref[:, start : start + pair]
        start += pair
        part = dot(hot, load[:pair])
        first = load[pair : pair + 1].astype(F32)
        second = load[pair + 1 : pair + 2].astype(F32)
        code = [
            jnp.broadcast_to(
                jnp.concatenate([first[:, lanes], second[:, lanes]], 1), (breadth // 2, pair)
            )
            for lanes in (slice(None, capacity), slice(capacity, None))
        ]
        count = dot(hot, jnp.concatenate(code, 0).astype(BF16), ((1,), (1,)))
        totals = part if totals is None else totals + part
        counts = count if counts is None else counts + count
    return totals, counts


def part_kernel(own_ref, near_ref, rowhot_ref, totals_ref, counts_ref):
    totals_ref[...], counts_ref[...] = load_totals(rowhot_ref, 0, [own_ref, near_ref])


def mean_kernel(totals_ref, counts_ref, rowhot_ref, *refs):
    loads, mean_ref = refs[:-1], refs[-1]
    breadth = mean_ref.shape[1]
    start = 4 * (loads[0].shape[0] // 2 - 1)
    totals, counts = load_totals(rowhot_ref, start, loads)
    totals = totals_ref[...] + totals
    counts = counts_ref[...] + counts
    counts = BASE * counts[:, : breadth // 2] + counts[:, breadth // 2 :]
    counts = jnp.concatenate([counts, counts], 1)
    mean = jnp.where(counts > 0.0, totals / jnp.maximum(counts, 1.0), -1.0)
    mean_ref[...] = mean.astype(BF16)


def gates(mean_code, gate_weight, update_bias):
    breadth = mean_code.shape[1]
    terms = dot(mean_code, gate_weight)
    update = jax.nn.sigmoid(terms[:, :breadth] + update_bias)
    candidate = jnp.tanh(terms[:, breadth:])
    touched = mean_code.astype(F32) >= 0.0
    keep_rate = jnp.where(touched, 1.0 - update, 1.0)
    write_term = jnp.where(touched, update * candidate, 0.0)
    return keep_rate, write_term


def gate_kernel(mean_ref, weight_ref, bias_ref, keep_ref, write_ref):
    keep_ref[...], write_ref[...] = gates(mean_ref[...], weight_ref[...], bias_ref[...])


def state_kernel(keep_all_ref, write_all_ref, memory_ref, weight_ref, bias_ref, *refs):
    periods = (len(refs) - 3) // 2 + 1
    means, outs, scratch = refs[: periods - 1], refs[periods - 1 : -3], refs[-3:]
    keep_ref, write_ref, state_ref = scratch
    me = lax.axis_index("tm")
    share = outs[0].shape[0]
    rows = pl.ds(pl.multiple_of(me * share, share), share)
    keep_ref[0], write_ref[0] = keep_all_ref[rows], write_all_ref[rows]
    for k, mean in enumerate(means):
        keep, write = gates(mean[...], weight_ref[...], bias_ref[...])
        keep_ref[k + 1], write_ref[k + 1] = keep, write
    state = memory_ref[rows]
    state_ref[0] = state
    for t in range(periods - 1):
        state = keep_ref[t ^ me] * state + write_ref[t ^ me]
        state_ref[t + 1] = state
    for k, out in enumerate(outs):
        out[...] = state_ref[me ^ k]


def final_kernel(keep_ref, write_ref, *refs):
    periods = (len(refs) - 3)
    befores, (out_any, made_ref, sems) = refs[:periods], refs[periods:]
    me = lax.axis_index("tm")
    share = befores[0].shape[0]
    copies = []
    for k, before in enumerate(befores):
        rows = pl.ds(pl.multiple_of((me ^ k) * share, share), share)
        made_ref[k] = keep_ref[rows] * before[...] + write_ref[rows]
        copies.append(pltpu.make_async_copy(made_ref.at[k], out_any.at[rows], sems.at[k]))
        copies[-1].start()
    for copy in copies:
        copy.wait()


def swap(axis, value, distance):
    size = lax.axis_size(axis)
    return lax.ppermute(value, axis, [(i, i ^ distance) for i in range(size)])


def shards(
    memory,
    src_slot,
    dst_slot,
    event_time,
    touched_rows,
    time_freq,
    msg_weight,
    msg_bias,
    gate_weight,
    update_bias,
):
    period = lax.axis_index("tm")
    periods = lax.axis_size("tm")
    blocks, capacity = touched_rows.shape[2:]
    node_rows, breadth = memory.shape
    events = src_slot.shape[2]
    chips = blocks // 2
    lists = jnp.maximum(touched_rows[0, 0], 0)

    pick_flops = chips * capacity * breadth * node_rows * 2
    other_picks, stale = call(
        fetch_kernel,
        [((chips, capacity, breadth), BF16), ((node_rows, breadth), BF16)],
        lists,
        memory,
        flops=pick_flops,
    )
    from_partner = swap("node", other_picks, 1)
    own = call(pick_kernel, [((chips, capacity, breadth), BF16)], lists, stale, flops=pick_flops)[0]
    sources, targets, times, from_partner = lax.optimization_barrier(
        (src_slot[0], dst_slot[0], event_time[0], from_partner)
    )
    tables = [own[0], from_partner[0]] + [
        swap("node", jnp.stack([own[chip], from_partner[chip]]), 2 * chip)
        for chip in range(1, chips)
    ]
    ends = 2 * events
    slots = blocks * capacity
    hot, turned, base, code = call(
        prep_kernel,
        [
            ((slots, ends), BF16),
            ((ends, slots), BF16),
            ((events, breadth), F32),
            ((blocks, 1, 2 * capacity), BF16),
        ],
        jnp.concatenate([sources, targets], 1),
        times,
        time_freq[None],
        msg_weight,
        msg_bias[None],
    )
    rows = call(
        gather_kernel,
        [((ends, breadth), F32)],
        *tables[:3],
        turned,
        flops=8 * ends * capacity * breadth,
    )[0]
    other, messages = call(
        message_kernel,
        [((chips, capacity + 1, breadth), BF16), ((ends, breadth), BF16)],
        rows,
        *tables[3:],
        turned,
        hot,
        msg_weight,
        base,
        code,
        flops=ends * slots * breadth * 3,
    )
    partner = swap("node", other, 1)
    own_sums = call(
        own_kernel,
        [((chips, capacity, breadth), BF16)],
        hot,
        messages,
        flops=ends * slots * breadth,
    )[0]
    loads = []
    for chip in range(chips):
        load = jnp.concatenate(
            [own_sums[chip], partner[chip, :capacity], code[2 * chip], partner[chip, capacity:]], 0
        )
        loads.append(swap("node", load, 2 * chip) if chip else load)
    rowhot = call(rows_kernel, [((node_rows, slots), BF16)], lists)[0]
    totals, counts = call(
        part_kernel,
        [((node_rows, breadth), F32)] * 2,
        *loads[:2],
        rowhot,
        flops=16 * node_rows * capacity * breadth,
    )
    mean_code = call(
        mean_kernel,
        [((node_rows, breadth), BF16)],
        totals,
        counts,
        rowhot,
        *loads[2:],
        flops=4 * node_rows * slots * breadth,
    )[0]

    share = node_rows // periods
    bias = update_bias[None]
    means = [
        swap("tm", lax.dynamic_slice_in_dim(mean_code, (period ^ k) * share, share, 0), k)
        for k in range(1, periods)
    ]
    keep, write = call(
        gate_kernel,
        [((node_rows, breadth), F32)] * 2,
        mean_code,
        gate_weight,
        bias,
        flops=4 * node_rows * breadth * breadth,
    )
    states = call(
        state_kernel,
        [((share, breadth), F32)] * periods,
        keep,
        write,
        memory,
        gate_weight,
        bias,
        *means,
        flops=4 * node_rows * breadth * breadth,
        scratch=[pltpu.VMEM((periods, share, breadth), F32)] * 3,
    )
    befores = [states[0]] + [
        swap("tm", states[k].astype(jnp.float16), k).astype(F32)
        for k in range(1, periods)
    ]
    result = call(
        final_kernel,
        [((node_rows, breadth), F32)],
        keep,
        write,
        *befores,
        scratch=[pltpu.VMEM((periods, share, breadth), F32), pltpu.SemaphoreType.DMA((periods,))],
        raw_out=(0,),
    )[0]
    return result[None]


def solution(mesh):
    return jax.shard_map(
        shards,
        mesh=mesh,
        in_specs=(
            P("node", None),
            P("tm", "node", None),
            P("tm", "node", None),
            P("tm", "node", None),
            P("tm", "node", None, None),
            P(),
            P(),
            P(),
            P(),
            P(),
        ),
        out_specs=P("tm", "node", None),
        check_vma=False,
    )
```

```python
import jax
import jax.numpy as jnp
from jax import lax
from jax.experimental import pallas as pl
from jax.experimental.pallas import tpu as pltpu
from jax.sharding import PartitionSpec as P

BASE = 32.0
WEIGHT = 16
VMEM_LIMIT = 20 << 20
F32 = jnp.float32
BF16 = jnp.bfloat16


def dot(a, b, dims=((1,), (0,))):
    return lax.dot_general(a, b, (dims, ((), ())), preferred_element_type=F32)


def call(kernel, outs, *args, flops=0, scratch=(), raw_out=()):
    outs = [jax.ShapeDtypeStruct(shape, dtype) for shape, dtype in outs]
    moved = sum(x.size * x.dtype.itemsize for x in [*args, *outs])

    def specs(count, raw):
        return [
            pl.BlockSpec(memory_space=pl.ANY if i in raw else pltpu.VMEM) for i in range(count)
        ]

    return pl.pallas_call(
        kernel,
        out_shape=outs,
        in_specs=specs(len(args), ()),
        out_specs=specs(len(outs), raw_out),
        scratch_shapes=list(scratch),
        cost_estimate=pl.CostEstimate(flops=WEIGHT * flops, bytes_accessed=moved, transcendentals=0),
        compiler_params=pltpu.CompilerParams(vmem_limit_bytes=VMEM_LIMIT),
    )(*args)


def columns_of(row):
    return jnp.transpose(jnp.broadcast_to(row, (row.shape[1], row.shape[1])))


def hot_rows(row, width):
    count = row.shape[1]
    column = jnp.concatenate([columns_of(row)] * (width // count), 1)
    lanes = lax.broadcasted_iota(jnp.int32, (count, width), 1)
    return jnp.where(column == lanes, 1.0, 0.0).astype(BF16)


def hot_columns(row, start, height):
    sublanes = lax.broadcasted_iota(jnp.int32, (height, row.shape[1]), 0) + start
    return jnp.where(row == sublanes, 1.0, 0.0).astype(BF16)


def lists_kernel(lists_ref, out_ref):
    out_ref[...] = lists_ref[...]


def picked(lists_ref, chip, stale):
    me = lax.axis_index("node")
    hot = hot_rows(lists_ref[pl.ds(me ^ (2 * chip), 1), :], stale.shape[0])
    return dot(hot, stale).astype(BF16)


def pick_kernel(lists_ref, memory_ref, out_ref):
    stale = memory_ref[...].astype(BF16)
    for chip in range(out_ref.shape[0]):
        out_ref[chip] = picked(lists_ref, chip, stale)


def pair_kernel(lists_ref, memory_ref, own_ref, *out_refs):
    stale = memory_ref[...].astype(BF16)
    for chip, out_ref in enumerate(out_refs):
        out_ref[0] = own_ref[chip]
        out_ref[1] = picked(lists_ref, chip, stale)


def prep_kernel(
    slots_ref, packed_ref, weight_ref, hot_ref, turned_ref, base_ref, code_ref, stale_weight_ref
):
    me = lax.axis_index("node")
    slots_all, ends = hot_ref.shape
    blocks, capacity = code_ref.shape[0], code_ref.shape[2] // 2
    slots = slots_ref[...]
    slots = ((slots // capacity) ^ me) * capacity + slots % capacity
    counts = jnp.zeros((8, slots_all), F32)
    ones = jnp.ones((8, capacity), BF16)
    for i in range(ends // capacity):
        rows = slice(i * capacity, (i + 1) * capacity)
        turned = hot_rows(slots[:, rows], slots_all)
        turned_ref[rows] = turned
        counts = counts + dot(ones, turned)
    for j in range(blocks):
        hot_ref[j * capacity : (j + 1) * capacity] = hot_columns(slots, j * capacity, capacity)
    upper = jnp.floor(counts * (1.0 / BASE))
    lower = counts - BASE * upper
    for j in range(blocks):
        lanes = slice(j * capacity, (j + 1) * capacity)
        code = jnp.concatenate([upper[:, lanes], lower[:, lanes]], 1)
        code_ref[j] = code[: code_ref.shape[1]].astype(BF16)
    events, _ = base_ref.shape
    stale_part = stale_weight_ref.shape[0]
    width = weight_ref.shape[0] - stale_part
    stale_weight_ref[...] = weight_ref[:stale_part]
    freq = packed_ref[:, events : events + width]
    bias = packed_ref[:, events + width :]
    for i in range(events // width):
        rows = slice(i * width, (i + 1) * width)
        encoding = jnp.cos(columns_of(packed_ref[:, rows]) * freq).astype(BF16)
        base_ref[rows] = dot(encoding, weight_ref[stale_part:]) + bias


def gathered(turned_ref, start, tables):
    rows = None
    for table in tables:
        stop = start + table.shape[0]
        part = dot(turned_ref[:, start:stop], table)
        rows = part if rows is None else rows + part
        start = stop
    return rows


def gather_kernel(own_ref, near_ref, turned_ref, rows_ref):
    _, capacity, breadth = own_ref.shape
    tables = [table[...].reshape(2 * capacity, breadth) for table in (own_ref, near_ref)]
    rows_ref[...] = gathered(turned_ref, 0, tables)


def message_kernel(rows_ref, *refs):
    tables, (turned_ref, hot_ref, weight_ref, base_ref, code_ref) = refs[:-7], refs[-7:-2]
    other_ref, message_ref = refs[-2:]
    _, capacity, breadth = tables[0].shape
    tables = [table[...].reshape(2 * capacity, breadth) for table in tables]
    rows = (rows_ref[...] + gathered(turned_ref, 4 * capacity, tables)).astype(BF16)
    events = rows.shape[0] // 2
    first = dot(rows, weight_ref[:breadth])
    second = dot(rows, weight_ref[breadth : 2 * breadth])
    base = base_ref[...]
    message_ref[:events] = jnp.maximum(first[:events] + second[events:] + base, 0.0).astype(BF16)
    message_ref[events:] = jnp.maximum(first[events:] + second[:events] + base, 0.0).astype(BF16)
    messages = message_ref[...]
    for chip in range(other_ref.shape[0]):
        j = 2 * chip + 1
        sums = dot(hot_ref[j * capacity : (j + 1) * capacity], messages)
        other_ref[chip, :capacity] = sums.astype(BF16)
        other_ref[chip, capacity:] = code_ref[j]


def own_kernel(hot_ref, message_ref, own_ref):
    messages = message_ref[...]
    chips, capacity, _ = own_ref.shape
    for chip in range(chips):
        rows = slice(2 * chip * capacity, (2 * chip + 1) * capacity)
        own_ref[chip] = dot(hot_ref[rows], messages).astype(BF16)


def rows_kernel(lists_ref, rowhot_ref):
    me = lax.axis_index("node")
    blocks, capacity = lists_ref.shape
    for j in range(blocks):
        row = lists_ref[pl.ds(me ^ j, 1), :]
        rowhot_ref[:, j * capacity : (j + 1) * capacity] = hot_columns(
            row, 0, rowhot_ref.shape[0]
        )


def load_totals(rowhot_ref, start, loads):
    totals, counts = None, None
    for load in loads:
        breadth = load.shape[1]
        pair = 2 * (load.shape[0] // 2 - 1)
        capacity = pair // 2
        hot = rowhot_ref[:, start : start + pair]
        start += pair
        part = dot(hot, load[:pair])
        first = load[pair : pair + 1].astype(F32)
        second = load[pair + 1 : pair + 2].astype(F32)
        code = [
            jnp.broadcast_to(
                jnp.concatenate([first[:, lanes], second[:, lanes]], 1), (breadth // 2, pair)
            )
            for lanes in (slice(None, capacity), slice(capacity, None))
        ]
        count = dot(hot, jnp.concatenate(code, 0).astype(BF16), ((1,), (1,)))
        totals = part if totals is None else totals + part
        counts = count if counts is None else counts + count
    return totals, counts


def part_kernel(own_ref, near_ref, rowhot_ref, totals_ref, counts_ref):
    totals_ref[...], counts_ref[...] = load_totals(rowhot_ref, 0, [own_ref, near_ref])


def mean_kernel(totals_ref, counts_ref, rowhot_ref, *refs):
    loads, mean_ref = refs[:-1], refs[-1]
    breadth = mean_ref.shape[1]
    start = 4 * (loads[0].shape[0] // 2 - 1)
    totals, counts = load_totals(rowhot_ref, start, loads)
    totals = totals_ref[...] + totals
    counts = counts_ref[...] + counts
    counts = BASE * counts[:, : breadth // 2] + counts[:, breadth // 2 :]
    counts = jnp.concatenate([counts, counts], 1)
    mean = jnp.where(counts > 0.0, totals / jnp.maximum(counts, 1.0), -1.0)
    mean_ref[...] = mean.astype(BF16)


def gates(mean_code, gate_weight, update_bias):
    breadth = mean_code.shape[1]
    terms = dot(mean_code, gate_weight)
    update = jax.nn.sigmoid(terms[:, :breadth] + update_bias)
    candidate = jnp.tanh(terms[:, breadth:])
    touched = mean_code.astype(F32) >= 0.0
    keep_rate = jnp.where(touched, 1.0 - update, 1.0)
    write_term = jnp.where(touched, update * candidate, 0.0)
    return keep_rate, write_term


def gate_kernel(mean_ref, weight_ref, bias_ref, keep_ref, write_ref):
    keep_ref[...], write_ref[...] = gates(mean_ref[...], weight_ref[...], bias_ref[...])


def state_kernel(keep_all_ref, write_all_ref, memory_ref, weight_ref, bias_ref, *refs):
    periods = (len(refs) - 3) // 2 + 1
    means, outs, scratch = refs[: periods - 1], refs[periods - 1 : -3], refs[-3:]
    keep_ref, write_ref, state_ref = scratch
    me = lax.axis_index("tm")
    share = outs[0].shape[0]
    rows = pl.ds(pl.multiple_of(me * share, share), share)
    keep_ref[0], write_ref[0] = keep_all_ref[rows], write_all_ref[rows]
    for k, mean in enumerate(means):
        keep, write = gates(mean[...], weight_ref[...], bias_ref[...])
        keep_ref[k + 1], write_ref[k + 1] = keep, write
    state = memory_ref[rows]
    state_ref[0] = state
    for t in range(periods - 1):
        state = keep_ref[t ^ me] * state + write_ref[t ^ me]
        state_ref[t + 1] = state
    for k, out in enumerate(outs):
        out[...] = state_ref[me ^ k]


def final_kernel(keep_ref, write_ref, *refs):
    periods = (len(refs) - 3)
    befores, (out_any, made_ref, sems) = refs[:periods], refs[periods:]
    me = lax.axis_index("tm")
    share = befores[0].shape[0]
    copies = []
    for k, before in enumerate(befores):
        rows = pl.ds(pl.multiple_of((me ^ k) * share, share), share)
        made_ref[k] = keep_ref[rows] * before[...] + write_ref[rows]
        copies.append(pltpu.make_async_copy(made_ref.at[k], out_any.at[rows], sems.at[k]))
        copies[-1].start()
    for copy in copies:
        copy.wait()


def swap(axis, value, distance):
    size = lax.axis_size(axis)
    return lax.ppermute(value, axis, [(i, i ^ distance) for i in range(size)])


def shards(
    memory,
    src_slot,
    dst_slot,
    event_time,
    touched_rows,
    time_freq,
    msg_weight,
    msg_bias,
    gate_weight,
    update_bias,
):
    period = lax.axis_index("tm")
    periods = lax.axis_size("tm")
    blocks, capacity = touched_rows.shape[2:]
    node_rows, breadth = memory.shape
    events = src_slot.shape[2]
    chips = blocks // 2
    lists = call(
        lists_kernel, [((blocks, capacity), jnp.int32)], touched_rows[0, 0], flops=1 << 26
    )[0]

    pick_flops = chips * capacity * breadth * node_rows * 2
    partner_memory = swap("node", memory, 1)
    partner_lists = swap("node", touched_rows[0, 0], 1)
    own = call(
        pick_kernel, [((chips, capacity, breadth), BF16)], lists, memory, flops=pick_flops
    )[0]
    tables = call(
        pair_kernel,
        [((2, capacity, breadth), BF16)] * chips,
        partner_lists,
        partner_memory,
        own,
        flops=pick_flops,
    )
    sources, targets, times = src_slot[0], dst_slot[0], event_time[0]
    tables = [swap("node", tables[chip], 2 * chip) if chip else tables[0] for chip in range(chips)]
    ends = 2 * events
    slots = blocks * capacity
    packed = jnp.concatenate([times, time_freq[None], msg_bias[None]], 1)
    slot_row = jnp.concatenate([sources, targets], 1)
    hot, turned, base, code, stale_weight = call(
        prep_kernel,
        [
            ((slots, ends), BF16),
            ((ends, slots), BF16),
            ((events, breadth), F32),
            ((blocks, 1, 2 * capacity), BF16),
            ((2 * breadth, breadth), BF16),
        ],
        slot_row,
        packed,
        msg_weight,
    )
    rows = call(
        gather_kernel,
        [((ends, breadth), F32)],
        *tables[:2],
        turned,
        flops=8 * ends * capacity * breadth,
    )[0]
    other, messages = call(
        message_kernel,
        [((chips, capacity + 1, breadth), BF16), ((ends, breadth), BF16)],
        rows,
        *tables[2:],
        turned,
        hot,
        stale_weight,
        base,
        code,
        flops=ends * slots * breadth * 3,
    )
    partner = swap("node", other, 1)
    own_sums = call(
        own_kernel,
        [((chips, capacity, breadth), BF16)],
        hot,
        messages,
        flops=ends * slots * breadth,
    )[0]
    loads = []
    for chip in range(chips):
        load = jnp.concatenate(
            [own_sums[chip], partner[chip, :capacity], code[2 * chip], partner[chip, capacity:]], 0
        )
        loads.append(swap("node", load, 2 * chip) if chip else load)
    rowhot = call(rows_kernel, [((node_rows, slots), BF16)], lists)[0]
    totals, counts = call(
        part_kernel,
        [((node_rows, breadth), F32)] * 2,
        *loads[:2],
        rowhot,
        flops=16 * node_rows * capacity * breadth,
    )
    mean_code = call(
        mean_kernel,
        [((node_rows, breadth), BF16)],
        totals,
        counts,
        rowhot,
        *loads[2:],
        flops=4 * node_rows * slots * breadth,
    )[0]

    share = node_rows // periods
    bias = update_bias[None]
    means = [
        swap("tm", lax.dynamic_slice_in_dim(mean_code, (period ^ k) * share, share, 0), k)
        for k in range(1, periods)
    ]
    keep, write = call(
        gate_kernel,
        [((node_rows, breadth), F32)] * 2,
        mean_code,
        gate_weight,
        bias,
        flops=4 * node_rows * breadth * breadth,
    )
    states = call(
        state_kernel,
        [((share, breadth), F32)] * periods,
        keep,
        write,
        memory,
        gate_weight,
        bias,
        *means,
        flops=4 * node_rows * breadth * breadth,
        scratch=[pltpu.VMEM((periods, share, breadth), F32)] * 3,
    )
    befores = [states[0]] + [
        swap("tm", states[k].astype(jnp.float16), k).astype(F32)
        for k in range(1, periods)
    ]
    result = call(
        final_kernel,
        [((node_rows, breadth), F32)],
        keep,
        write,
        *befores,
        scratch=[pltpu.VMEM((periods, share, breadth), F32), pltpu.SemaphoreType.DMA((periods,))],
        raw_out=(0,),
    )[0]
    return result[None]


def solution(mesh):
    return jax.shard_map(
        shards,
        mesh=mesh,
        in_specs=(
            P("node", None),
            P("tm", "node", None),
            P("tm", "node", None),
            P("tm", "node", None),
            P("tm", "node", None, None),
            P(),
            P(),
            P(),
            P(),
            P(),
        ),
        out_specs=P("tm", "node", None),
        check_vma=False,
    )
```

```python
import jax
import jax.numpy as jnp
from jax import lax
from jax.experimental import pallas as pl
from jax.experimental.pallas import tpu as pltpu
from jax.sharding import PartitionSpec as P

BASE = 32.0
WEIGHT = 16
VMEM_LIMIT = 20 << 20
F32 = jnp.float32
BF16 = jnp.bfloat16


def dot(a, b, dims=((1,), (0,))):
    return lax.dot_general(a, b, (dims, ((), ())), preferred_element_type=F32)


def call(kernel, outs, *args, flops=0, scratch=(), raw_in=(), raw_out=(), aliases={}):
    outs = [jax.ShapeDtypeStruct(shape, dtype) for shape, dtype in outs]
    moved = sum(x.size * x.dtype.itemsize for x in [*args, *outs])

    def specs(count, raw):
        return [
            pl.BlockSpec(memory_space=pl.ANY if i in raw else pltpu.VMEM) for i in range(count)
        ]

    return pl.pallas_call(
        kernel,
        out_shape=outs,
        in_specs=specs(len(args), raw_in),
        out_specs=specs(len(outs), raw_out),
        scratch_shapes=list(scratch),
        input_output_aliases=aliases,
        cost_estimate=pl.CostEstimate(flops=WEIGHT * flops, bytes_accessed=moved, transcendentals=0),
        compiler_params=pltpu.CompilerParams(vmem_limit_bytes=VMEM_LIMIT),
    )(*args)


def columns_of(row):
    return jnp.transpose(jnp.broadcast_to(row, (row.shape[1], row.shape[1])))


def hot_rows(row, width):
    count = row.shape[1]
    column = jnp.concatenate([columns_of(row)] * (width // count), 1)
    lanes = lax.broadcasted_iota(jnp.int32, (count, width), 1)
    return jnp.where(column == lanes, 1.0, 0.0).astype(BF16)


def hot_columns(row, start, height):
    sublanes = lax.broadcasted_iota(jnp.int32, (height, row.shape[1]), 0) + start
    return jnp.where(row == sublanes, 1.0, 0.0).astype(BF16)


def lists_kernel(lists_ref, out_ref):
    out_ref[...] = lists_ref[...]


def picked(lists_ref, chip, stale):
    me = lax.axis_index("node")
    hot = hot_rows(lists_ref[pl.ds(me ^ (2 * chip), 1), :], stale.shape[0])
    return dot(hot, stale).astype(BF16)


def pick_kernel(lists_ref, memory_ref, out_ref):
    stale = memory_ref[...].astype(BF16)
    for chip in range(out_ref.shape[0]):
        out_ref[chip] = picked(lists_ref, chip, stale)


def pair_kernel(lists_ref, memory_ref, own_ref, *out_refs):
    stale = memory_ref[...].astype(BF16)
    for chip, out_ref in enumerate(out_refs):
        out_ref[0] = own_ref[chip]
        out_ref[1] = picked(lists_ref, chip, stale)


def prep_kernel(
    slots_ref, packed_ref, weight_ref, hot_ref, turned_ref, base_ref, code_ref, stale_weight_ref
):
    me = lax.axis_index("node")
    slots_all, ends = hot_ref.shape
    blocks, capacity = code_ref.shape[0], code_ref.shape[2] // 2
    slots = slots_ref[...]
    slots = ((slots // capacity) ^ me) * capacity + slots % capacity
    counts = jnp.zeros((8, slots_all), F32)
    ones = jnp.ones((8, capacity), BF16)
    for i in range(ends // capacity):
        rows = slice(i * capacity, (i + 1) * capacity)
        turned = hot_rows(slots[:, rows], slots_all)
        turned_ref[rows] = turned
        counts = counts + dot(ones, turned)
    for j in range(blocks):
        hot_ref[j * capacity : (j + 1) * capacity] = hot_columns(slots, j * capacity, capacity)
    upper = jnp.floor(counts * (1.0 / BASE))
    lower = counts - BASE * upper
    for j in range(blocks):
        lanes = slice(j * capacity, (j + 1) * capacity)
        code = jnp.concatenate([upper[:, lanes], lower[:, lanes]], 1)
        code_ref[j] = code[: code_ref.shape[1]].astype(BF16)
    events, _ = base_ref.shape
    stale_part = stale_weight_ref.shape[0]
    width = weight_ref.shape[0] - stale_part
    stale_weight_ref[...] = weight_ref[:stale_part]
    freq = packed_ref[:, events : events + width]
    bias = packed_ref[:, events + width :]
    for i in range(events // width):
        rows = slice(i * width, (i + 1) * width)
        encoding = jnp.cos(columns_of(packed_ref[:, rows]) * freq).astype(BF16)
        base_ref[rows] = dot(encoding, weight_ref[stale_part:]) + bias


def gathered(turned_ref, start, tables):
    rows = None
    for table in tables:
        stop = start + table.shape[0]
        part = dot(turned_ref[:, start:stop], table)
        rows = part if rows is None else rows + part
        start = stop
    return rows


def gather_kernel(own_ref, near_ref, turned_ref, rows_ref):
    _, capacity, breadth = own_ref.shape
    tables = [table[...].reshape(2 * capacity, breadth) for table in (own_ref, near_ref)]
    rows_ref[...] = gathered(turned_ref, 0, tables)


def message_kernel(rows_ref, *refs):
    tables, (turned_ref, hot_ref, weight_ref, base_ref, code_ref) = refs[:-7], refs[-7:-2]
    other_ref, message_ref = refs[-2:]
    _, capacity, breadth = tables[0].shape
    tables = [table[...].reshape(2 * capacity, breadth) for table in tables]
    rows = (rows_ref[...] + gathered(turned_ref, 4 * capacity, tables)).astype(BF16)
    events = rows.shape[0] // 2
    first = dot(rows, weight_ref[:breadth])
    second = dot(rows, weight_ref[breadth : 2 * breadth])
    base = base_ref[...]
    message_ref[:events] = jnp.maximum(first[:events] + second[events:] + base, 0.0).astype(BF16)
    message_ref[events:] = jnp.maximum(first[events:] + second[:events] + base, 0.0).astype(BF16)
    messages = message_ref[...]
    for chip in range(other_ref.shape[0]):
        j = 2 * chip + 1
        sums = dot(hot_ref[j * capacity : (j + 1) * capacity], messages)
        other_ref[chip, :capacity] = sums.astype(BF16)
        other_ref[chip, capacity:] = code_ref[j]


def own_kernel(hot_ref, message_ref, own_ref):
    messages = message_ref[...]
    chips, capacity, _ = own_ref.shape
    for chip in range(chips):
        rows = slice(2 * chip * capacity, (2 * chip + 1) * capacity)
        own_ref[chip] = dot(hot_ref[rows], messages).astype(BF16)


def rows_kernel(lists_ref, rowhot_ref):
    me = lax.axis_index("node")
    blocks, capacity = lists_ref.shape
    for j in range(blocks):
        row = lists_ref[pl.ds(me ^ j, 1), :]
        rowhot_ref[:, j * capacity : (j + 1) * capacity] = hot_columns(
            row, 0, rowhot_ref.shape[0]
        )


def load_totals(rowhot_ref, start, loads):
    totals, counts = None, None
    for load in loads:
        breadth = load.shape[1]
        pair = 2 * (load.shape[0] // 2 - 1)
        capacity = pair // 2
        hot = rowhot_ref[:, start : start + pair]
        start += pair
        part = dot(hot, load[:pair])
        first = load[pair : pair + 1].astype(F32)
        second = load[pair + 1 : pair + 2].astype(F32)
        code = [
            jnp.broadcast_to(
                jnp.concatenate([first[:, lanes], second[:, lanes]], 1), (breadth // 2, pair)
            )
            for lanes in (slice(None, capacity), slice(capacity, None))
        ]
        count = dot(hot, jnp.concatenate(code, 0).astype(BF16), ((1,), (1,)))
        totals = part if totals is None else totals + part
        counts = count if counts is None else counts + count
    return totals, counts


def part_kernel(own_ref, near_ref, rowhot_ref, totals_ref, counts_ref):
    totals_ref[...], counts_ref[...] = load_totals(rowhot_ref, 0, [own_ref, near_ref])


def mean_kernel(totals_ref, counts_ref, rowhot_ref, *refs):
    loads, mean_ref = refs[:-1], refs[-1]
    breadth = mean_ref.shape[1]
    start = 4 * (loads[0].shape[0] // 2 - 1)
    totals, counts = load_totals(rowhot_ref, start, loads)
    totals = totals_ref[...] + totals
    counts = counts_ref[...] + counts
    counts = BASE * counts[:, : breadth // 2] + counts[:, breadth // 2 :]
    counts = jnp.concatenate([counts, counts], 1)
    mean = jnp.where(counts > 0.0, totals / jnp.maximum(counts, 1.0), -1.0)
    mean_ref[...] = mean.astype(BF16)


def gates(mean_code, gate_weight, update_bias):
    breadth = mean_code.shape[1]
    terms = dot(mean_code, gate_weight)
    update = jax.nn.sigmoid(terms[:, :breadth] + update_bias)
    candidate = jnp.tanh(terms[:, breadth:])
    touched = mean_code.astype(F32) >= 0.0
    keep_rate = jnp.where(touched, 1.0 - update, 1.0)
    write_term = jnp.where(touched, update * candidate, 0.0)
    return keep_rate, write_term


def gate_kernel(mean_ref, weight_ref, bias_ref, keep_ref, write_ref):
    keep_ref[...], write_ref[...] = gates(mean_ref[...], weight_ref[...], bias_ref[...])


def state_kernel(keep_all_ref, write_all_ref, memory_ref, weight_ref, bias_ref, *refs):
    periods = (len(refs) - 3) // 2 + 1
    means, outs, scratch = refs[: periods - 1], refs[periods - 1 : -3], refs[-3:]
    keep_ref, write_ref, state_ref = scratch
    me = lax.axis_index("tm")
    share = outs[0].shape[0]
    rows = pl.ds(pl.multiple_of(me * share, share), share)
    keep_ref[0], write_ref[0] = keep_all_ref[rows], write_all_ref[rows]
    for k, mean in enumerate(means):
        keep, write = gates(mean[...], weight_ref[...], bias_ref[...])
        keep_ref[k + 1], write_ref[k + 1] = keep, write
    state = memory_ref[rows]
    state_ref[0] = state
    for t in range(periods - 1):
        state = keep_ref[t ^ me] * state + write_ref[t ^ me]
        state_ref[t + 1] = state
    for k, out in enumerate(outs):
        out[...] = state_ref[me ^ k]


def share_copy(keep_ref, write_ref, before, k, made_ref, out_any, sems):
    share = made_ref.shape[1]
    start = (lax.axis_index("tm") ^ k) * share
    rows = pl.ds(pl.multiple_of(start, share), share)
    made_ref[k] = keep_ref[rows] * before(rows) + write_ref[rows]
    return pltpu.make_async_copy(made_ref.at[k], out_any.at[rows], sems.at[k])


def early_kernel(keep_ref, write_ref, memory_ref, own_ref, out_any, made_ref, sems):
    own = share_copy(keep_ref, write_ref, lambda rows: own_ref[...], 0, made_ref, out_any, sems)
    own.start()

    @pl.when(lax.axis_index("tm") == 0)
    def _():
        copies = []
        for k in range(1, made_ref.shape[0]):
            before = lambda rows: memory_ref[rows]
            copies.append(share_copy(keep_ref, write_ref, before, k, made_ref, out_any, sems))
            copies[-1].start()
        for copy in copies:
            copy.wait()

    own.wait()


def final_kernel(keep_ref, write_ref, *refs):
    befores, (prior_any, out_any, made_ref, sems) = refs[:-4], refs[-4:]
    del prior_any

    @pl.when(lax.axis_index("tm") != 0)
    def _():
        copies = []
        for k, came in enumerate(befores, 1):
            before = lambda rows, came=came: came[...]
            copies.append(share_copy(keep_ref, write_ref, before, k, made_ref, out_any, sems))
            copies[-1].start()
        for copy in copies:
            copy.wait()


def swap(axis, value, distance):
    size = lax.axis_size(axis)
    return lax.ppermute(value, axis, [(i, i ^ distance) for i in range(size)])


def shards(
    memory,
    src_slot,
    dst_slot,
    event_time,
    touched_rows,
    time_freq,
    msg_weight,
    msg_bias,
    gate_weight,
    update_bias,
):
    period = lax.axis_index("tm")
    periods = lax.axis_size("tm")
    blocks, capacity = touched_rows.shape[2:]
    node_rows, breadth = memory.shape
    events = src_slot.shape[2]
    chips = blocks // 2
    lists = call(
        lists_kernel, [((blocks, capacity), jnp.int32)], touched_rows[0, 0], flops=1 << 26
    )[0]

    pick_flops = chips * capacity * breadth * node_rows * 2
    partner_memory = swap("node", memory, 1)
    partner_lists = swap("node", touched_rows[0, 0], 1)
    own = call(
        pick_kernel, [((chips, capacity, breadth), BF16)], lists, memory, flops=pick_flops
    )[0]
    tables = call(
        pair_kernel,
        [((2, capacity, breadth), BF16)] * chips,
        partner_lists,
        partner_memory,
        own,
        flops=pick_flops,
    )
    sources, targets, times = src_slot[0], dst_slot[0], event_time[0]
    tables = [swap("node", tables[chip], 2 * chip) if chip else tables[0] for chip in range(chips)]
    ends = 2 * events
    slots = blocks * capacity
    packed = jnp.concatenate([times, time_freq[None], msg_bias[None]], 1)
    slot_row = jnp.concatenate([sources, targets], 1)
    hot, turned, base, code, stale_weight = call(
        prep_kernel,
        [
            ((slots, ends), BF16),
            ((ends, slots), BF16),
            ((events, breadth), F32),
            ((blocks, 1, 2 * capacity), BF16),
            ((2 * breadth, breadth), BF16),
        ],
        slot_row,
        packed,
        msg_weight,
    )
    rows = call(
        gather_kernel,
        [((ends, breadth), F32)],
        *tables[:2],
        turned,
        flops=8 * ends * capacity * breadth,
    )[0]
    other, messages = call(
        message_kernel,
        [((chips, capacity + 1, breadth), BF16), ((ends, breadth), BF16)],
        rows,
        *tables[2:],
        turned,
        hot,
        stale_weight,
        base,
        code,
        flops=ends * slots * breadth * 3,
    )
    partner = swap("node", other, 1)
    own_sums = call(
        own_kernel,
        [((chips, capacity, breadth), BF16)],
        hot,
        messages,
        flops=ends * slots * breadth,
    )[0]
    loads = []
    for chip in range(chips):
        load = jnp.concatenate(
            [own_sums[chip], partner[chip, :capacity], code[2 * chip], partner[chip, capacity:]], 0
        )
        loads.append(swap("node", load, 2 * chip) if chip else load)
    rowhot = call(rows_kernel, [((node_rows, slots), BF16)], lists)[0]
    totals, counts = call(
        part_kernel,
        [((node_rows, breadth), F32)] * 2,
        *loads[:2],
        rowhot,
        flops=16 * node_rows * capacity * breadth,
    )
    mean_code = call(
        mean_kernel,
        [((node_rows, breadth), BF16)],
        totals,
        counts,
        rowhot,
        *loads[2:],
        flops=4 * node_rows * slots * breadth,
    )[0]

    share = node_rows // periods
    bias = update_bias[None]
    means = [
        swap("tm", lax.dynamic_slice_in_dim(mean_code, (period ^ k) * share, share, 0), k)
        for k in range(1, periods)
    ]
    keep, write = call(
        gate_kernel,
        [((node_rows, breadth), F32)] * 2,
        mean_code,
        gate_weight,
        bias,
        flops=4 * node_rows * breadth * breadth,
    )
    states = call(
        state_kernel,
        [((share, breadth), F32)] * periods,
        keep,
        write,
        memory,
        gate_weight,
        bias,
        *means,
        flops=4 * node_rows * breadth * breadth,
        scratch=[pltpu.VMEM((periods, share, breadth), F32)] * 3,
    )
    befores = [swap("tm", states[k].astype(jnp.float16), k).astype(F32) for k in range(1, periods)]
    made = [pltpu.VMEM((periods, share, breadth), F32), pltpu.SemaphoreType.DMA((periods,))]
    early = call(
        early_kernel,
        [((node_rows, breadth), F32)],
        keep,
        write,
        memory,
        states[0],
        scratch=made,
        raw_out=(0,),
        flops=4 * node_rows * breadth,
    )[0]
    result = call(
        final_kernel,
        [((node_rows, breadth), F32)],
        keep,
        write,
        *befores,
        early,
        scratch=made,
        raw_in=(periods + 1,),
        raw_out=(0,),
        aliases={periods + 1: 0},
    )[0]
    return result[None]


def solution(mesh):
    return jax.shard_map(
        shards,
        mesh=mesh,
        in_specs=(
            P("node", None),
            P("tm", "node", None),
            P("tm", "node", None),
            P("tm", "node", None),
            P("tm", "node", None, None),
            P(),
            P(),
            P(),
            P(),
            P(),
        ),
        out_specs=P("tm", "node", None),
        check_vma=False,
    )
```

```python
import functools

import jax
import jax.numpy as jnp
from jax import lax
from jax.experimental import pallas as pl
from jax.experimental.pallas import tpu as pltpu
from jax.sharding import PartitionSpec as P

BASE = 32.0
WEIGHT = 16
VMEM_LIMIT = 20 << 20
F32 = jnp.float32
BF16 = jnp.bfloat16


def dot(a, b, dims=((1,), (0,))):
    return lax.dot_general(a, b, (dims, ((), ())), preferred_element_type=F32)


def call(kernel, outs, *args, flops=0, scratch=(), raw_in=(), raw_out=(), aliases={}):
    outs = [jax.ShapeDtypeStruct(shape, dtype) for shape, dtype in outs]
    moved = sum(x.size * x.dtype.itemsize for x in [*args, *outs])

    def specs(count, raw):
        return [
            pl.BlockSpec(memory_space=pl.ANY if i in raw else pltpu.VMEM) for i in range(count)
        ]

    return pl.pallas_call(
        kernel,
        out_shape=outs,
        in_specs=specs(len(args), raw_in),
        out_specs=specs(len(outs), raw_out),
        scratch_shapes=list(scratch),
        input_output_aliases=aliases,
        cost_estimate=pl.CostEstimate(flops=WEIGHT * flops, bytes_accessed=moved, transcendentals=0),
        compiler_params=pltpu.CompilerParams(vmem_limit_bytes=VMEM_LIMIT),
    )(*args)


def columns_of(row):
    return jnp.transpose(jnp.broadcast_to(row, (row.shape[1], row.shape[1])))


def hot_rows(row, width):
    count = row.shape[1]
    column = jnp.concatenate([columns_of(row)] * (width // count), 1)
    lanes = lax.broadcasted_iota(jnp.int32, (count, width), 1)
    return jnp.where(column == lanes, 1.0, 0.0).astype(BF16)


def hot_columns(row, start, height):
    sublanes = lax.broadcasted_iota(jnp.int32, (height, row.shape[1]), 0) + start
    return jnp.where(row == sublanes, 1.0, 0.0).astype(BF16)


def lists_kernel(lists_ref, out_ref):
    out_ref[...] = lists_ref[...]


def picked(lists_ref, chip, stale):
    me = lax.axis_index("node")
    hot = hot_rows(lists_ref[pl.ds(me ^ (2 * chip), 1), :], stale.shape[0])
    return dot(hot, stale).astype(BF16)


def pick_kernel(lists_ref, memory_ref, out_ref):
    stale = memory_ref[...].astype(BF16)
    for chip in range(out_ref.shape[0]):
        out_ref[chip] = picked(lists_ref, chip, stale)


def pair_kernel(lists_ref, memory_ref, own_ref, *out_refs):
    stale = memory_ref[...].astype(BF16)
    for chip, out_ref in enumerate(out_refs):
        out_ref[0] = own_ref[chip]
        out_ref[1] = picked(lists_ref, chip, stale)


def prep_kernel(
    slots_ref, packed_ref, weight_ref, hot_ref, turned_ref, base_ref, code_ref, stale_weight_ref
):
    me = lax.axis_index("node")
    slots_all, ends = hot_ref.shape
    blocks, capacity = code_ref.shape[0], code_ref.shape[2] // 2
    slots = slots_ref[...]
    slots = ((slots // capacity) ^ me) * capacity + slots % capacity
    counts = jnp.zeros((8, slots_all), F32)
    ones = jnp.ones((8, capacity), BF16)
    for i in range(ends // capacity):
        rows = slice(i * capacity, (i + 1) * capacity)
        turned = hot_rows(slots[:, rows], slots_all)
        turned_ref[rows] = turned
        counts = counts + dot(ones, turned)
    for j in range(blocks):
        hot_ref[j * capacity : (j + 1) * capacity] = hot_columns(slots, j * capacity, capacity)
    upper = jnp.floor(counts * (1.0 / BASE))
    lower = counts - BASE * upper
    for j in range(blocks):
        lanes = slice(j * capacity, (j + 1) * capacity)
        code = jnp.concatenate([upper[:, lanes], lower[:, lanes]], 1)
        code_ref[j] = code[: code_ref.shape[1]].astype(BF16)
    events, _ = base_ref.shape
    stale_part = stale_weight_ref.shape[0]
    width = weight_ref.shape[0] - stale_part
    stale_weight_ref[...] = weight_ref[:stale_part]
    freq = packed_ref[:, events : events + width]
    bias = packed_ref[:, events + width :]
    for i in range(events // width):
        rows = slice(i * width, (i + 1) * width)
        encoding = jnp.cos(columns_of(packed_ref[:, rows]) * freq).astype(BF16)
        base_ref[rows] = dot(encoding, weight_ref[stale_part:]) + bias


def gathered(turned_ref, start, tables):
    rows = None
    for table in tables:
        stop = start + table.shape[0]
        part = dot(turned_ref[:, start:stop], table)
        rows = part if rows is None else rows + part
        start = stop
    return rows


def gather_kernel(own_ref, near_ref, turned_ref, rows_ref):
    _, capacity, breadth = own_ref.shape
    tables = [table[...].reshape(2 * capacity, breadth) for table in (own_ref, near_ref)]
    rows_ref[...] = gathered(turned_ref, 0, tables)


def other_sums(chosen, hot_ref, messages, code_ref, out_ref):
    capacity = code_ref.shape[2] // 2
    for i, chip in enumerate(chosen):
        j = 2 * chip + 1
        sums = dot(hot_ref[j * capacity : (j + 1) * capacity], messages)
        out_ref[i, :capacity] = sums.astype(BF16)
        out_ref[i, capacity:] = code_ref[j]


def message_kernel(rows_ref, *refs):
    tables, (turned_ref, hot_ref, weight_ref, base_ref, code_ref) = refs[:-7], refs[-7:-2]
    other_ref, message_ref = refs[-2:]
    _, capacity, breadth = tables[0].shape
    tables = [table[...].reshape(2 * capacity, breadth) for table in tables]
    rows = (rows_ref[...] + gathered(turned_ref, 4 * capacity, tables)).astype(BF16)
    events = rows.shape[0] // 2
    first = dot(rows, weight_ref[:breadth])
    second = dot(rows, weight_ref[breadth : 2 * breadth])
    base = base_ref[...]
    message_ref[:events] = jnp.maximum(first[:events] + second[events:] + base, 0.0).astype(BF16)
    message_ref[events:] = jnp.maximum(first[events:] + second[:events] + base, 0.0).astype(BF16)
    other_sums([1], hot_ref, message_ref[...], code_ref, other_ref)


def rest_kernel(chosen, hot_ref, message_ref, code_ref, other_ref):
    other_sums(chosen, hot_ref, message_ref[...], code_ref, other_ref)


def own_kernel(hot_ref, message_ref, own_ref):
    messages = message_ref[...]
    chips, capacity, _ = own_ref.shape
    for chip in range(chips):
        rows = slice(2 * chip * capacity, (2 * chip + 1) * capacity)
        own_ref[chip] = dot(hot_ref[rows], messages).astype(BF16)


def rows_kernel(lists_ref, rowhot_ref):
    me = lax.axis_index("node")
    blocks, capacity = lists_ref.shape
    for j in range(blocks):
        row = lists_ref[pl.ds(me ^ j, 1), :]
        rowhot_ref[:, j * capacity : (j + 1) * capacity] = hot_columns(
            row, 0, rowhot_ref.shape[0]
        )


def load_totals(rowhot_ref, start, loads):
    totals, counts = None, None
    for load in loads:
        breadth = load.shape[1]
        pair = 2 * (load.shape[0] // 2 - 1)
        capacity = pair // 2
        hot = rowhot_ref[:, start : start + pair]
        start += pair
        part = dot(hot, load[:pair])
        first = load[pair : pair + 1].astype(F32)
        second = load[pair + 1 : pair + 2].astype(F32)
        code = [
            jnp.broadcast_to(
                jnp.concatenate([first[:, lanes], second[:, lanes]], 1), (breadth // 2, pair)
            )
            for lanes in (slice(None, capacity), slice(capacity, None))
        ]
        count = dot(hot, jnp.concatenate(code, 0).astype(BF16), ((1,), (1,)))
        totals = part if totals is None else totals + part
        counts = count if counts is None else counts + count
    return totals, counts


def part_kernel(own_ref, near_ref, rowhot_ref, totals_ref, counts_ref):
    totals_ref[...], counts_ref[...] = load_totals(rowhot_ref, 0, [own_ref, near_ref])


def mean_kernel(totals_ref, counts_ref, rowhot_ref, *refs):
    loads, mean_ref = refs[:-1], refs[-1]
    breadth = mean_ref.shape[1]
    start = 4 * (loads[0].shape[0] // 2 - 1)
    totals, counts = load_totals(rowhot_ref, start, loads)
    totals = totals_ref[...] + totals
    counts = counts_ref[...] + counts
    counts = BASE * counts[:, : breadth // 2] + counts[:, breadth // 2 :]
    counts = jnp.concatenate([counts, counts], 1)
    mean = jnp.where(counts > 0.0, totals / jnp.maximum(counts, 1.0), -1.0)
    mean_ref[...] = mean.astype(BF16)


def gates(mean_code, gate_weight, update_bias):
    breadth = mean_code.shape[1]
    terms = dot(mean_code, gate_weight)
    update = jax.nn.sigmoid(terms[:, :breadth] + update_bias)
    candidate = jnp.tanh(terms[:, breadth:])
    touched = mean_code.astype(F32) >= 0.0
    keep_rate = jnp.where(touched, 1.0 - update, 1.0)
    write_term = jnp.where(touched, update * candidate, 0.0)
    return keep_rate, write_term


def gate_kernel(mean_ref, weight_ref, bias_ref, keep_ref, write_ref):
    keep_ref[...], write_ref[...] = gates(mean_ref[...], weight_ref[...], bias_ref[...])


def state_kernel(keep_all_ref, write_all_ref, memory_ref, weight_ref, bias_ref, *refs):
    periods = (len(refs) - 3) // 2 + 1
    means, outs, scratch = refs[: periods - 1], refs[periods - 1 : -3], refs[-3:]
    keep_ref, write_ref, state_ref = scratch
    me = lax.axis_index("tm")
    share = outs[0].shape[0]
    rows = pl.ds(pl.multiple_of(me * share, share), share)
    keep_ref[0], write_ref[0] = keep_all_ref[rows], write_all_ref[rows]
    for k, mean in enumerate(means):
        keep, write = gates(mean[...], weight_ref[...], bias_ref[...])
        keep_ref[k + 1], write_ref[k + 1] = keep, write
    state = memory_ref[rows]
    state_ref[0] = state
    for t in range(periods - 1):
        state = keep_ref[t ^ me] * state + write_ref[t ^ me]
        state_ref[t + 1] = state
    for k, out in enumerate(outs):
        out[...] = state_ref[me ^ k]


def share_copy(keep_ref, write_ref, before, k, made_ref, out_any, sems):
    share = made_ref.shape[1]
    start = (lax.axis_index("tm") ^ k) * share
    rows = pl.ds(pl.multiple_of(start, share), share)
    made_ref[k] = keep_ref[rows] * before(rows) + write_ref[rows]
    return pltpu.make_async_copy(made_ref.at[k], out_any.at[rows], sems.at[k])


def early_kernel(keep_ref, write_ref, memory_ref, own_ref, out_any, made_ref, sems):
    own = share_copy(keep_ref, write_ref, lambda rows: own_ref[...], 0, made_ref, out_any, sems)
    own.start()

    @pl.when(lax.axis_index("tm") == 0)
    def _():
        copies = []
        for k in range(1, made_ref.shape[0]):
            before = lambda rows: memory_ref[rows]
            copies.append(share_copy(keep_ref, write_ref, before, k, made_ref, out_any, sems))
            copies[-1].start()
        for copy in copies:
            copy.wait()

    own.wait()


def final_kernel(keep_ref, write_ref, *refs):
    befores, (prior_any, out_any, made_ref, sems) = refs[:-4], refs[-4:]
    del prior_any

    @pl.when(lax.axis_index("tm") != 0)
    def _():
        copies = []
        for k, came in enumerate(befores, 1):
            before = lambda rows, came=came: came[...]
            copies.append(share_copy(keep_ref, write_ref, before, k, made_ref, out_any, sems))
            copies[-1].start()
        for copy in copies:
            copy.wait()


def swap(axis, value, distance):
    size = lax.axis_size(axis)
    return lax.ppermute(value, axis, [(i, i ^ distance) for i in range(size)])


def shards(
    memory,
    src_slot,
    dst_slot,
    event_time,
    touched_rows,
    time_freq,
    msg_weight,
    msg_bias,
    gate_weight,
    update_bias,
):
    period = lax.axis_index("tm")
    periods = lax.axis_size("tm")
    blocks, capacity = touched_rows.shape[2:]
    node_rows, breadth = memory.shape
    events = src_slot.shape[2]
    chips = blocks // 2
    lists = call(
        lists_kernel, [((blocks, capacity), jnp.int32)], touched_rows[0, 0], flops=1 << 26
    )[0]

    pick_flops = chips * capacity * breadth * node_rows * 2
    partner_memory = swap("node", memory, 1)
    partner_lists = swap("node", touched_rows[0, 0], 1)
    own = call(
        pick_kernel, [((chips, capacity, breadth), BF16)], lists, memory, flops=pick_flops
    )[0]
    tables = call(
        pair_kernel,
        [((2, capacity, breadth), BF16)] * chips,
        partner_lists,
        partner_memory,
        own,
        flops=pick_flops,
    )
    sources, targets, times = src_slot[0], dst_slot[0], event_time[0]
    tables = [swap("node", tables[chip], 2 * chip) if chip else tables[0] for chip in range(chips)]
    ends = 2 * events
    slots = blocks * capacity
    packed = jnp.concatenate([times, time_freq[None], msg_bias[None]], 1)
    slot_row = jnp.concatenate([sources, targets], 1)
    hot, turned, base, code, stale_weight = call(
        prep_kernel,
        [
            ((slots, ends), BF16),
            ((ends, slots), BF16),
            ((events, breadth), F32),
            ((blocks, 1, 2 * capacity), BF16),
            ((2 * breadth, breadth), BF16),
        ],
        slot_row,
        packed,
        msg_weight,
    )
    rows = call(
        gather_kernel,
        [((ends, breadth), F32)],
        *tables[:2],
        turned,
        flops=8 * ends * capacity * breadth,
    )[0]
    other, messages = call(
        message_kernel,
        [((1, capacity + 1, breadth), BF16), ((ends, breadth), BF16)],
        rows,
        *tables[2:],
        turned,
        hot,
        stale_weight,
        base,
        code,
        flops=ends * slots * breadth * 3,
    )
    chosen = [chip for chip in range(chips) if chip != 1]
    rest = call(
        functools.partial(rest_kernel, chosen),
        [((chips - 1, capacity + 1, breadth), BF16)],
        hot,
        messages,
        code,
        flops=ends * slots * breadth,
    )[0]
    came = swap("node", other, 1)
    rest = swap("node", rest, 1)
    partner = {1: came[0]} | {chip: rest[i] for i, chip in enumerate(chosen)}
    own_sums = call(
        own_kernel,
        [((chips, capacity, breadth), BF16)],
        hot,
        messages,
        flops=ends * slots * breadth,
    )[0]
    loads = []
    for chip in range(chips):
        theirs = partner[chip]
        load = jnp.concatenate(
            [own_sums[chip], theirs[:capacity], code[2 * chip], theirs[capacity:]], 0
        )
        loads.append(swap("node", load, 2 * chip) if chip else load)
    rowhot = call(rows_kernel, [((node_rows, slots), BF16)], lists)[0]
    totals, counts = call(
        part_kernel,
        [((node_rows, breadth), F32)] * 2,
        *loads[:2],
        rowhot,
        flops=16 * node_rows * capacity * breadth,
    )
    mean_code = call(
        mean_kernel,
        [((node_rows, breadth), BF16)],
        totals,
        counts,
        rowhot,
        *loads[2:],
        flops=4 * node_rows * slots * breadth,
    )[0]

    share = node_rows // periods
    bias = update_bias[None]
    means = [
        swap("tm", lax.dynamic_slice_in_dim(mean_code, (period ^ k) * share, share, 0), k)
        for k in range(1, periods)
    ]
    keep, write = call(
        gate_kernel,
        [((node_rows, breadth), F32)] * 2,
        mean_code,
        gate_weight,
        bias,
        flops=4 * node_rows * breadth * breadth,
    )
    states = call(
        state_kernel,
        [((share, breadth), F32)] * periods,
        keep,
        write,
        memory,
        gate_weight,
        bias,
        *means,
        flops=4 * node_rows * breadth * breadth,
        scratch=[pltpu.VMEM((periods, share, breadth), F32)] * 3,
    )
    befores = [swap("tm", states[k].astype(jnp.float16), k).astype(F32) for k in range(1, periods)]
    made = [pltpu.VMEM((periods, share, breadth), F32), pltpu.SemaphoreType.DMA((periods,))]
    early = call(
        early_kernel,
        [((node_rows, breadth), F32)],
        keep,
        write,
        memory,
        states[0],
        scratch=made,
        raw_out=(0,),
        flops=4 * node_rows * breadth,
    )[0]
    result = call(
        final_kernel,
        [((node_rows, breadth), F32)],
        keep,
        write,
        *befores,
        early,
        scratch=made,
        raw_in=(periods + 1,),
        raw_out=(0,),
        aliases={periods + 1: 0},
    )[0]
    return result[None]


def solution(mesh):
    return jax.shard_map(
        shards,
        mesh=mesh,
        in_specs=(
            P("node", None),
            P("tm", "node", None),
            P("tm", "node", None),
            P("tm", "node", None),
            P("tm", "node", None, None),
            P(),
            P(),
            P(),
            P(),
            P(),
        ),
        out_specs=P("tm", "node", None),
        check_vma=False,
    )
```
